32 devices in a mesh: dp: 8 (over z, x), tensor: 4 (over y, core).
Axes of the slice: x: 2, y: 2, z: 4, core: 2. Of those that a mesh axis runs over, the one named last changes fastest.
Arguments:
- layer_in: bfloat16 [16, 729, 1152], P('dp'), may hold values from -6 to 6
- first_norm_gain: float32 [1152], replicated, may hold values from 0.1 to 1.9
- first_norm_bias: float32 [1152], replicated, may hold values from -3 to 3
- w_qkv: bfloat16 [1152, 3, 1152], P(None, None, 'tensor'), may hold values from -0.1875 to 0.1875
- b_q: float32 [1152], P('tensor'), may hold values from -3 to 3
- b_v: float32 [1152], P('tensor'), may hold values from -3 to 3
- w_out: bfloat16 [1152, 1152], P('tensor'), may hold values from -1 to 1
- b_out: float32 [1152], replicated, may hold values from -4 to 4
- second_norm_gain: float32 [1152], replicated, may hold values from 0.1 to 1.9
- second_norm_bias: float32 [1152], replicated, may hold values from -3 to 3
- w_up: bfloat16 [1152, 4304], P(None, 'tensor'), may hold values from -0.1875 to 0.1875
- b_up: float32 [4304], P('tensor'), may hold values from -3 to 3
- w_down: bfloat16 [4304, 1152], P('tensor'), may hold values from -0.375 to 0.375
- b_down: float32 [1152], replicated, may hold values from -4 to 4
- cotangent: bfloat16 [16, 729, 1152], P('dp'), may hold values from -6 to 6
Outputs:
- layer_out: float32 [16, 729, 1152], P('dp')
- grad_x: float32 [16, 729, 1152], P('dp')
- grad_ln1_gain: float32 [1152], replicated
- grad_ln1_bias: float32 [1152], replicated
- grad_w_qkv: float32 [1152, 3, 1152], P(None, None, 'tensor')
- grad_b_q: float32 [1152], P('tensor')
- grad_b_v: float32 [1152], P('tensor')
- grad_w_out: float32 [1152, 1152], P('tensor')
- grad_b_out: float32 [1152], replicated
- grad_ln2_gain: float32 [1152], replicated
- grad_ln2_bias: float32 [1152], replicated
- grad_w_up: float32 [1152, 4304], P(None, 'tensor')
- grad_b_up: float32 [4304], P('tensor')
- grad_w_down: float32 [4304, 1152], P('tensor')
- grad_b_down: float32 [1152], replicated
The draws below stay inside these ranges and needn't reach their ends.
All inputs are finite; a program needn't handle non-finite values.
Results may differ from the reference program's by a relative error of at most 0.019.
Values may be sent and summed in bfloat16 or wider, within the bound.
No kernel may reach another device: no remote copies, remote signals or barrier semaphores. Data moves between devices by JAX's collectives and lax.ppermute only.
A program may use at most 256 MiB of HBM per device.

```python
import jax
import jax.numpy as jnp
from jax import lax

D = 1152
HEADS = 16
HD = 72
FF = 4304
SEQ = 729
IMAGES = 16
N_TENSOR = 4


def steps_of(own_key, extent, shards, low, largest):
    level, own = 1.0, jax.random.fold_in(own_key, 6)
    for position, shards_of in shards:
        heights = jnp.exp(jax.random.uniform(jax.random.fold_in(own, position), (shards_of,), jnp.float32, low / len(shards), largest / len(shards)))
        level = level * jnp.repeat(heights, extent[position] // shards_of).reshape([-1 if axis == position else 1 for axis in range(len(extent))])
    return level


def scatter_about(rng, shape, spread, most, shards=(), kind=jnp.bfloat16):
    drawn = jax.random.normal(rng, shape, jnp.float32) * spread
    if len(shards) > 0:
        drawn = steps_of(rng, shape, shards, -0.22, 0.18) * drawn
    return jnp.clip(drawn, min=-most, max=most).astype(kind)


def setup_inputs(seed: int = 0) -> dict:
    streams_of = jax.random.split(jax.random.key(seed), 16)
    return {
        "layer_in": scatter_about(streams_of[0], (IMAGES, SEQ, D), 1.0, 6.0, ((0, 8),)),
        "first_norm_gain": jnp.clip(1.0 + 0.18 * jax.random.normal(streams_of[1], (D,), jnp.float32), 0.1, 1.9),
        "first_norm_bias": scatter_about(streams_of[2], (D,), 0.6, 3.0, (), jnp.float32),
        "w_qkv": scatter_about(streams_of[3], (D, 3, D), D ** -0.5, 0.1875, ((2, 4),)),
        "b_q": scatter_about(streams_of[4], (D,), 0.5, 3.0, ((0, 4),), jnp.float32),
        "b_v": scatter_about(streams_of[5], (D,), 0.5, 3.0, ((0, 4),), jnp.float32),
        "w_out": scatter_about(streams_of[6], (D, D), (D // 32) ** -0.5, 1.0, ((0, 4),)),
        "b_out": scatter_about(streams_of[7], (D,), 1.0, 4.0, (), jnp.float32),
        "second_norm_gain": jnp.clip(1.0 + 0.18 * jax.random.normal(streams_of[8], (D,), jnp.float32), 0.1, 1.9),
        "second_norm_bias": scatter_about(streams_of[9], (D,), 0.6, 3.0, (), jnp.float32),
        "w_up": scatter_about(streams_of[10], (D, FF), D ** -0.5, 0.1875, ((1, 4),)),
        "b_up": scatter_about(streams_of[11], (FF,), 0.5, 3.0, ((0, 4),), jnp.float32),
        "w_down": scatter_about(streams_of[12], (FF, D), (FF // 16) ** -0.5, 0.375, ((0, 4),)),
        "b_down": scatter_about(streams_of[13], (D,), 1.0, 4.0, (), jnp.float32),
        "cotangent": scatter_about(streams_of[14], (IMAGES, SEQ, D), 1.0, 6.0, ((0, 8),)),
    }


EPSILON = 1e-06
GELU_C = 0.7978845608028654

def apply_layer_norm(values_in, gain, shift):
    center = values_in - lax.optimization_barrier(jnp.mean(values_in, axis=-1, keepdims=True))
    variance = lax.optimization_barrier(jnp.mean(center * center, axis=-1, keepdims=True))
    inv_std = lax.rsqrt(variance + EPSILON)
    x_hat = center * inv_std
    return (x_hat * gain + shift, x_hat, inv_std)

def norm_gradient_pass(d_normed, x_hat, inv_std, gain):
    scaled = d_normed * gain
    return inv_std * (scaled - lax.optimization_barrier(jnp.mean(scaled, axis=-1, keepdims=True)) - x_hat * lax.optimization_barrier(jnp.mean(scaled * x_hat, axis=-1, keepdims=True)))

def gelu_parts(pre_act):
    inner = GELU_C * (pre_act + 0.044715 * pre_act * pre_act * pre_act)
    tangent = jnp.tanh(inner)
    value = 0.5 * pre_act * (1.0 + tangent)
    slope = 0.5 * (1.0 + tangent) + 0.5 * pre_act * (1.0 - tangent * tangent) * GELU_C * (1.0 + 3.0 * 0.044715 * pre_act * pre_act)
    return (value, slope)

def rounded(values_in):
    return lax.optimization_barrier(values_in.astype(jnp.bfloat16)).astype(jnp.float32)

def reference(layer_in, first_norm_gain, first_norm_bias, w_qkv, b_q, b_v, w_out, b_out, second_norm_gain, second_norm_bias, w_up, b_up, w_down, b_down, cotangent):
    groups = N_TENSOR
    group_width = D // groups
    group_units = FF // groups
    scaling = HD ** (-0.5)

    def one_image(carry, inputs):
        image_in, cotan_in = inputs
        input_row_block = image_in.astype(jnp.float32)
        first_normalized_rows, first_standardized, first_inverse_deviation = apply_layer_norm(input_row_block, first_norm_gain, first_norm_bias)
        first_normalized_rows = first_normalized_rows.astype(jnp.bfloat16)
        projected = jnp.dot(first_normalized_rows, w_qkv.reshape(D, 3 * D), preferred_element_type=jnp.float32).reshape(SEQ, 3, D)
        queries = (projected[:, 0] + b_q).astype(jnp.bfloat16)
        keys_all = projected[:, 1].astype(jnp.bfloat16)
        values_all = (projected[:, 2] + b_v).astype(jnp.bfloat16)
        query_heads = queries.astype(jnp.float32).reshape(SEQ, HEADS, HD)
        key_heads = keys_all.astype(jnp.float32).reshape(SEQ, HEADS, HD)
        value_heads = values_all.astype(jnp.float32).reshape(SEQ, HEADS, HD)
        scores = jnp.einsum('shd,thd->hst', query_heads, key_heads) * scaling
        logsum = jax.nn.logsumexp(scores, axis=-1)
        softmax_f = jnp.exp(scores - logsum[..., None])
        probs_b = softmax_f.astype(jnp.bfloat16)
        attended = jnp.einsum('hst,thd->shd', probs_b.astype(jnp.float32), value_heads).reshape(SEQ, D).astype(jnp.bfloat16)
        partials = jnp.einsum('sgc,gcd->gsd', attended.astype(jnp.float32).reshape(SEQ, groups, group_width), w_out.astype(jnp.float32).reshape(groups, group_width, D))
        attn_sum = lax.optimization_barrier(jnp.sum(rounded(partials), axis=0))
        first_residual_rows = input_row_block + attn_sum + b_out
        second_normalized_rows, second_standardized, second_inverse_deviation = apply_layer_norm(first_residual_rows, second_norm_gain, second_norm_bias)
        second_normalized_rows = second_normalized_rows.astype(jnp.bfloat16)
        pre_act = jnp.dot(second_normalized_rows, w_up, preferred_element_type=jnp.float32) + b_up
        act_value, act_slope = gelu_parts(pre_act)
        activated = act_value.astype(jnp.bfloat16)
        mlp_parts = jnp.einsum('sgf,gfd->gsd', activated.astype(jnp.float32).reshape(SEQ, groups, group_units), w_down.astype(jnp.float32).reshape(groups, group_units, D))
        mlp_sum = lax.optimization_barrier(jnp.sum(rounded(mlp_parts), axis=0))
        output = first_residual_rows + mlp_sum + b_down
        cotangent_row_block = cotan_in.astype(jnp.float32)
        grad_bdown = lax.optimization_barrier(jnp.sum(cotangent_row_block, axis=0))
        grad_wdown = jnp.dot(activated.T, cotan_in, preferred_element_type=jnp.float32)
        d_pre = jnp.dot(cotan_in, w_down.T, preferred_element_type=jnp.float32) * act_slope
        grad_bup = lax.optimization_barrier(jnp.sum(d_pre, axis=0))
        d_pre_b = d_pre.astype(jnp.bfloat16)
        grad_wup = jnp.dot(second_normalized_rows.T, d_pre_b, preferred_element_type=jnp.float32)
        back_parts = jnp.einsum('sgf,egf->gse', d_pre_b.astype(jnp.float32).reshape(SEQ, groups, group_units), w_up.astype(jnp.float32).reshape(D, groups, group_units))
        second_norm_gradient = lax.optimization_barrier(jnp.sum(rounded(back_parts), axis=0))
        second_gain_gradient = lax.optimization_barrier(jnp.sum(second_norm_gradient * second_standardized, axis=0))
        grad_c2 = lax.optimization_barrier(jnp.sum(second_norm_gradient, axis=0))
        residual_gradient = norm_gradient_pass(second_norm_gradient, second_standardized, second_inverse_deviation, second_norm_gain) + cotangent_row_block
        grad_bout = lax.optimization_barrier(jnp.sum(residual_gradient, axis=0))
        d_resid_b = residual_gradient.astype(jnp.bfloat16)
        grad_wout = jnp.dot(attended.T, d_resid_b, preferred_element_type=jnp.float32)
        d_attended = jnp.dot(d_resid_b, w_out.T, preferred_element_type=jnp.float32).astype(jnp.bfloat16)
        d_att_heads = d_attended.astype(jnp.float32).reshape(SEQ, HEADS, HD)
        d_probs = jnp.einsum('shd,thd->hst', d_att_heads, value_heads)
        d_values = jnp.einsum('hst,shd->thd', probs_b.astype(jnp.float32), d_att_heads).reshape(SEQ, D)
        delta = lax.optimization_barrier(jnp.sum(softmax_f * d_probs, axis=-1, keepdims=True))
        d_scores = (softmax_f * (d_probs - delta) * scaling).astype(jnp.bfloat16).astype(jnp.float32)
        d_queries = jnp.einsum('hst,thd->shd', d_scores, key_heads).reshape(SEQ, D)
        d_keys = jnp.einsum('hst,shd->thd', d_scores, query_heads).reshape(SEQ, D)
        grad_bq = lax.optimization_barrier(jnp.sum(d_queries, axis=0))
        grad_bv = lax.optimization_barrier(jnp.sum(d_values, axis=0))
        d_qkv = jnp.stack([d_queries, d_keys, d_values], axis=1).astype(jnp.bfloat16)
        grad_wqkv = jnp.einsum('se,stc->etc', first_normalized_rows.astype(jnp.float32), d_qkv.astype(jnp.float32))
        first_parts = jnp.einsum('stgc,etgc->gse', d_qkv.astype(jnp.float32).reshape(SEQ, 3, groups, group_width), w_qkv.astype(jnp.float32).reshape(D, 3, groups, group_width))
        first_norm_gradient = lax.optimization_barrier(jnp.sum(rounded(first_parts), axis=0))
        first_gain_gradient = lax.optimization_barrier(jnp.sum(first_norm_gradient * first_standardized, axis=0))
        grad_c1 = lax.optimization_barrier(jnp.sum(first_norm_gradient, axis=0))
        input_gradient = norm_gradient_pass(first_norm_gradient, first_standardized, first_inverse_deviation, first_norm_gain) + residual_gradient
        terms = (first_gain_gradient, grad_c1, grad_wqkv, grad_bq, grad_bv, grad_wout, grad_bout, second_gain_gradient, grad_c2, grad_wup, grad_bup, grad_wdown, grad_bdown)
        carry = tuple((total + term for total, term in zip(carry, terms)))
        return (carry, (output, input_gradient))
    zeros_init = (jnp.zeros((D,), jnp.float32), jnp.zeros((D,), jnp.float32), jnp.zeros((D, 3, D), jnp.float32), jnp.zeros((D,), jnp.float32), jnp.zeros((D,), jnp.float32), jnp.zeros((D, D), jnp.float32), jnp.zeros((D,), jnp.float32), jnp.zeros((D,), jnp.float32), jnp.zeros((D,), jnp.float32), jnp.zeros((D, FF), jnp.float32), jnp.zeros((FF,), jnp.float32), jnp.zeros((FF, D), jnp.float32), jnp.zeros((D,), jnp.float32))
    totals, (outputs, grads_in) = lax.scan(one_image, zeros_init, (layer_in, cotangent))
    return (outputs, grads_in) + tuple(totals)
```

```python
import jax
import jax.numpy as jnp
from jax import lax
from jax.sharding import Mesh, PartitionSpec as P

HD = 72
EPSILON = 1e-06
GELU_C = 0.7978845608028654
F32 = jnp.float32
BF16 = jnp.bfloat16


def round_up(value, multiple):
    return -(-value // multiple) * multiple


def dot(a, b, contract):
    return lax.dot_general(a, b, ((contract[:1], contract[1:]), ((), ())), preferred_element_type=F32)


def norm_statistics(v):
    center = v - jnp.mean(v, axis=-1, keepdims=True)
    inv_std = lax.rsqrt(jnp.mean(center * center, axis=-1, keepdims=True) + EPSILON)
    return center * inv_std, inv_std


def norm_gradient(d_normed, x_hat, inv_std, gain):
    e = d_normed * gain
    return inv_std * (
        e - jnp.mean(e, axis=-1, keepdims=True) - x_hat * jnp.mean(e * x_hat, axis=-1, keepdims=True)
    )


def gelu_parts(u):
    t = jnp.tanh(GELU_C * (u + 0.044715 * u * u * u))
    value = 0.5 * u * (1.0 + t)
    slope = 0.5 * (1.0 + t) + 0.5 * u * (1.0 - t * t) * GELU_C * (1.0 + 3.0 * 0.044715 * u * u)
    return value, slope


def swap(value, axis, distance=1):
    size = lax.axis_size(axis)
    return lax.ppermute(value, axis, [(k, k ^ distance) for k in range(size)])


def add(a, b):
    return (a.astype(F32) + b.astype(F32)).astype(BF16)


def tensor_sum(keep, send):
    pair = add(keep, swap(send, "c"))
    own = add(pair, swap(pair, "y"))
    return own, swap(own, "c")


def halves(part, core):
    half = part.shape[0] // 2
    keep = lax.dynamic_slice_in_dim(part, core * half, half, 0)
    send = lax.dynamic_slice_in_dim(part, (1 - core) * half, half, 0)
    return keep, send


def join(own, other, index):
    first = jnp.where(index == 0, own, other)
    second = jnp.where(index == 0, other, own)
    return first, second


def outer_sum(value, level=1):
    size = lax.axis_size("o")
    if level >= size:
        return value
    if level * 2 >= size:
        return add(value, swap(value, "o", level))
    bit = (lax.axis_index("o") // level) % 2
    half = value.shape[0] // 2
    keep, send = halves(value, bit)
    mine = outer_sum(add(keep, swap(send, "o", level)), level * 2)
    return jnp.concatenate(join(mine, swap(mine, "o", level), bit), axis=0)


def grads_sum(keep, send):
    mine = outer_sum(add(keep, swap(send, "i")))
    return mine, swap(mine, "i")


def small_sum(value, axes):
    for axis in axes:
        level = 1
        while level < lax.axis_size(axis):
            value = value + swap(value, axis, level)
            level *= 2
    return value


def attention_forward(x, g1, c1, w_t, b_q, b_v, w_out, core):
    rows, width = x.shape
    local = b_q.shape[0]
    heads = local // HD
    x_hat, _ = norm_statistics(x.astype(F32))
    n1 = (x_hat * g1 + c1).astype(BF16)
    q = (dot(w_t[0], n1, (1, 1)) + b_q[:, None]).astype(BF16)
    k = dot(w_t[1], n1, (1, 1)).astype(BF16)
    v = (dot(w_t[2], n1, (1, 1)) + b_v[:, None]).astype(BF16)
    qh, kh, vh = (t.reshape(heads, HD, rows) for t in (q, k, v))
    s = jnp.einsum("hdk,hdq->hkq", kh, qh, preferred_element_type=F32) * (HD ** (-0.5))
    lse = jax.nn.logsumexp(s, axis=1)
    p = jnp.exp(s - lse[:, None]).astype(BF16)
    att = jnp.einsum("hdk,hkq->hdq", vh, p, preferred_element_type=F32).astype(BF16).reshape(local, rows)
    part = dot(att, w_out, (0, 0)).astype(BF16)
    part = jnp.pad(part, ((0, round_up(rows, 32) - rows), (0, 0)))
    return n1, (q, k, v), att, lse, halves(part, core)


def residual(x, sums, b_out, core):
    first, second = join(*sums, core)
    attn_sum = jnp.concatenate([first, second], axis=0)[: x.shape[0]]
    return x.astype(F32) + attn_sum.astype(F32) + b_out


def feed_forward(x, cot, attn_sums, b_out, g2, c2, w_up_t, b_up, w_down, core):
    rows = x.shape[0]
    x_hat, _ = norm_statistics(residual(x, attn_sums, b_out, core))
    n2 = (x_hat * g2 + c2).astype(BF16)
    pre = dot(w_up_t, n2, (1, 1)) + b_up[:, None]
    value, slope = gelu_parts(pre)
    act = value.astype(BF16)
    d_pre = dot(w_down, cot, (1, 1)) * slope
    g_bup = jnp.sum(d_pre, axis=1)
    d_pre = d_pre.astype(BF16)
    pad = ((0, round_up(rows, 32) - rows), (0, 0))
    back = jnp.pad(dot(d_pre, w_up_t, (0, 0)).astype(BF16), pad)
    return n2, act, d_pre, g_bup, halves(back, core)


def feed_forward_out(act, w_down, core):
    rows = act.shape[1]
    pad = ((0, round_up(rows, 32) - rows), (0, 0))
    return halves(jnp.pad(dot(act, w_down, (0, 0)).astype(BF16), pad), core)


def attention_backward(x, cot, attn_sums, b_out, g2, back_sums, n1, qkv, att, lse, w_t, w_out, g1, core):
    rows, width = x.shape
    q, k, v = qkv
    local = q.shape[0]
    heads = local // HD
    x_hat, inv_std = norm_statistics(residual(x, attn_sums, b_out, core))
    first, second = join(*back_sums, core)
    dn = jnp.concatenate([first, second], axis=0)[:rows].astype(F32)
    g_ln2 = jnp.sum(dn * x_hat, axis=0), jnp.sum(dn, axis=0)
    dr = norm_gradient(dn, x_hat, inv_std, g2) + cot.astype(F32)
    g_bout = jnp.sum(dr, axis=0)
    dr_b = dr.astype(BF16)
    d_att = dot(w_out, dr_b, (1, 1)).astype(BF16)
    qh, kh, vh, oh, doh = (t.reshape(heads, HD, rows) for t in (q, k, v, att, d_att))
    scale = HD ** (-0.5)
    s = jnp.einsum("hdk,hdq->hkq", kh, qh, preferred_element_type=F32) * scale
    p = jnp.exp(s - lse[:, None])
    dp = jnp.einsum("hdk,hdq->hkq", vh, doh, preferred_element_type=F32)
    delta = jnp.sum(p * dp, axis=1)
    ds = (p * (dp - delta[:, None]) * scale).astype(BF16)
    dv = jnp.einsum("hdq,hkq->hdk", doh, p.astype(BF16), preferred_element_type=F32).reshape(local, rows)
    dk = jnp.einsum("hdq,hkq->hdk", qh, ds, preferred_element_type=F32).reshape(local, rows)
    dq = jnp.einsum("hdk,hkq->hdq", kh, ds, preferred_element_type=F32).reshape(local, rows)
    g_bq, g_bv = jnp.sum(dq, axis=1), jnp.sum(dv, axis=1)
    d_qkv = jnp.concatenate([dq, dk, dv], axis=0).astype(BF16)
    part = dot(d_qkv, w_t.reshape(3 * local, width), (0, 0)).astype(BF16)
    x_hat1, _ = norm_statistics(x.astype(F32))
    part_f = part.astype(F32)
    g_ln1 = jnp.sum(part_f * x_hat1, axis=0), jnp.sum(part_f, axis=0)
    part = jnp.pad(part, ((0, round_up(rows, 32) - rows), (0, 0)))
    return dr, dr_b, d_qkv, g_ln2, g_bout, g_bq, g_bv, g_ln1, halves(part, core)


def per_device(
    layer_in, g1, c1, w_qkv, b_q, b_v, w_out, b_out, g2, c2, w_up, b_up, w_down, b_down, cotangent
):
    images, rows, width = layer_in.shape
    local, units = b_q.shape[0], b_up.shape[0]
    core, inner = lax.axis_index("c"), lax.axis_index("i")
    w_t = w_qkv.transpose(1, 2, 0)
    w_up_t = w_up.T
    xs = [layer_in[k] for k in range(images)]
    cots = [cotangent[k] for k in range(images)]
    span = range(images)

    fwd = [attention_forward(x, g1, c1, w_t, b_q, b_v, w_out, core) for x in xs]
    attn_sums = [tensor_sum(*f[4]) for f in fwd]
    g_bdown = sum(jnp.sum(c.astype(F32), axis=0) for c in cots)
    ff = [feed_forward(xs[k], cots[k], attn_sums[k], b_out, g2, c2, w_up_t, b_up, w_down, core) for k in span]
    back_sums = [tensor_sum(*f[4]) for f in ff]
    mlp_sums = [tensor_sum(*feed_forward_out(f[1], w_down, core)) for f in ff]

    pad = ((0, round_up(units, 64) - units), (0, 0))
    g_down = sum(dot(ff[k][1], cots[k], (1, 0)) for k in span)
    g_up = sum(dot(ff[k][2], ff[k][0], (1, 0)) for k in span)
    g_ff = jnp.stack([jnp.pad(g.astype(BF16), pad) for g in (g_down, g_up)])
    keep = lax.dynamic_index_in_dim(g_ff, inner, 0, keepdims=False)
    send = lax.dynamic_index_in_dim(g_ff, 1 - inner, 0, keepdims=False)
    g_down, g_up = (g[:units].astype(F32) for g in join(*grads_sum(keep, send), inner))

    bwd = [
        attention_backward(
            xs[k], cots[k], attn_sums[k], b_out, g2, back_sums[k], fwd[k][0], fwd[k][1], fwd[k][2], fwd[k][3],
            w_t, w_out, g1, core,
        )
        for k in span
    ]
    in_sums = [tensor_sum(*b[8]) for b in bwd]
    g_qkv = sum(dot(bwd[k][2], fwd[k][0], (1, 0)) for k in span)
    g_out = sum(dot(fwd[k][2], bwd[k][1], (1, 0)) for k in span)
    g_attn = jnp.concatenate([g_qkv, g_out], axis=0).astype(BF16).reshape(2, 2 * local, width)
    keep = lax.dynamic_index_in_dim(g_attn, inner, 0, keepdims=False)
    send = lax.dynamic_index_in_dim(g_attn, 1 - inner, 0, keepdims=False)
    g_attn = jnp.concatenate(join(*grads_sum(keep, send), inner), axis=0).astype(F32)

    def total(values):
        values = list(values)
        return sum(values[1:], values[0])

    def row(v):
        return jnp.pad(v, (0, width - v.shape[0]))

    ln1 = jnp.stack([total(b[7][0] for b in bwd), total(b[7][1] for b in bwd)])
    ln1 = small_sum(ln1, ("c", "y"))
    rest = jnp.stack(
        [
            g_bdown,
            row(total(f[3] for f in ff)),
            total(b[3][0] for b in bwd),
            total(b[3][1] for b in bwd),
            total(b[4] for b in bwd),
            row(jnp.concatenate([total(b[5] for b in bwd), total(b[6] for b in bwd)])),
        ]
    )
    small = small_sum(jnp.concatenate([ln1, rest], axis=0), ("i", "o"))

    outs, grads = [], []
    for k in span:
        resid = residual(xs[k], attn_sums[k], b_out, core)
        outs.append(residual_like(resid, mlp_sums[k], core) + b_down)
        x_hat, inv_std = norm_statistics(xs[k].astype(F32))
        dn = residual_like(0.0, in_sums[k], core, rows)
        grads.append(norm_gradient(dn, x_hat, inv_std, g1) + bwd[k][0])
    return (
        jnp.stack(outs),
        jnp.stack(grads),
        small[0],
        small[1],
        g_attn[: 3 * local].reshape(3, local, width).transpose(2, 0, 1),
        small[7][:local],
        small[7][local : 2 * local],
        g_attn[3 * local :],
        small[6],
        small[4],
        small[5],
        g_up.T,
        small[3][:units],
        g_down,
        small[2],
    )


def residual_like(base, sums, core, rows=None):
    both = jnp.concatenate(join(*sums, core), axis=0).astype(F32)
    return base + both[: base.shape[0] if rows is None else rows]


def solution(mesh):
    dp, tensor = mesh.devices.shape
    fine = Mesh(mesh.devices.reshape(dp // 2, 2, tensor // 2, 2), ("o", "i", "y", "c"))
    D, T = ("o", "i"), ("y", "c")
    in_specs = (
        P(D, None, None), P(), P(), P(None, None, T), P(T), P(T), P(T, None), P(), P(), P(),
        P(None, T), P(T), P(T, None), P(), P(D, None, None),
    )
    out_specs = (
        P(D, None, None), P(D, None, None), P(), P(), P(None, None, T), P(T), P(T), P(T, None), P(), P(), P(),
        P(None, T), P(T), P(T, None), P(),
    )
    return jax.shard_map(per_device, mesh=fine, in_specs=in_specs, out_specs=out_specs, check_vma=False)
```
